32 devices in a mesh: groups: 2 (over y), ctx: 8 (over z, x), head: 2 (over core).
Axes of the slice: x: 2, y: 2, z: 4, core: 2. Of those that a mesh axis runs over, the one named last changes fastest.
Arguments:
- queries: bfloat16 [2048, 2048], P(('groups', 'ctx'), 'head'), parts along dimension 0, may hold values from -80 to 80
- keys: bfloat16 [2048, 512], P(('groups', 'ctx'), 'head'), parts along dimension 0, may hold values from -6 to 6
- values: bfloat16 [2048, 512], P(('groups', 'ctx'), 'head'), parts along dimension 0, may hold values from -6 to 6
- pattern: int32 [16, 8], P(('groups', 'ctx')), parts along dimension 0, may hold values from -1 to 7, as said below
- x_in: bfloat16 [2048, 1024], P(('groups', 'ctx'), 'head'), parts along dimension 0, may hold values from -2 to 2
- z_gate: bfloat16 [2048, 1024], P(('groups', 'ctx'), 'head'), parts along dimension 0, may hold values from -6 to 6
- bmat: bfloat16 [2048, 256], P(('groups', 'ctx'), 'head'), parts along dimension 0, may hold values from -6 to 6
- cmat: bfloat16 [2048, 256], P(('groups', 'ctx'), 'head'), parts along dimension 0, may hold values from -0.5 to 0.5
- log_decay: float32 [32, 1024], P(('groups', 'head'), 'ctx'), parts along dimension 0, may hold values from -2 to 0
- gain: float32 [1024], P('head'), may hold values from 0.1 to 1.9
Outputs:
- attn_out: bfloat16 [2048, 2048], P(('groups', 'ctx'), 'head'), parts along dimension 0
- ssm_out: bfloat16 [2048, 1024], P(('groups', 'ctx'), 'head'), parts along dimension 0
The draws below stay inside these ranges and needn't reach their ends.
There are 2 independent parts, one for each index of `groups`. The reference program is written for one: setup_inputs(seed, part) draws one part's arguments, and reference() takes and returns one part's arrays. A program takes and returns all parts, laid end to end along the dimension named above; an argument that names none is the same for every part. Nothing has to cross between parts.
Inputs may be any that keep to these rules, and one draw needn't show every extreme that they name: `pattern`: entry 0 of row q is q; the other entries are distinct blocks from q - 3 to q - 1, or -1 where no block is listed.
All inputs are finite; a program needn't handle non-finite values.
Results may differ from the reference program's by a relative error of at most 0.009.
Values may be sent and summed in bfloat16 or wider, within the bound.
No kernel may reach another device: no remote copies, remote signals or barrier semaphores. Data moves between devices by JAX's collectives and lax.ppermute only.
A program may use at most 128 MiB of HBM per device.

```python
import jax
import jax.numpy as jnp
from jax import lax

BLK = 128
SCAN_BLK = 128
HD = 128
KVH = 4
QPK = 4
P_SIZE = 64
N = 128
HG = 8
SG = 2
KSEL = 8
MH = 16
TOKENS = 1024
NB = 8
WIN = 3


def head_speeds(key):
    inner = jax.random.fold_in(key, 7)
    pick_key, level_key = jax.random.split(inner)
    slow_share = 0.5
    slow_heads = jax.random.uniform(pick_key, (MH,)) < slow_share
    level = jax.random.uniform(level_key, (MH,))
    slow_rate = 0.3 * 2.0 ** level / TOKENS
    quick_speed = 2.4 ** level / 60.0
    return jnp.where(slow_heads, slow_rate, quick_speed)


def key_field(key):
    inner = jax.random.fold_in(key, 31)
    field = jnp.clip(jax.random.normal(inner, (NB, BLK, KVH * HD)), -6.0, 6.0)
    return field


def draw_keys(key, part):
    return key_field(key).reshape(TOKENS, KVH * HD).astype(jnp.bfloat16)


def draw_queries(key, part):
    inner = jax.random.fold_in(key, 37)
    field = jnp.clip(jax.random.normal(inner, (NB, BLK, KVH, QPK, HD)), -6.0, 6.0)
    return field.reshape(TOKENS, KVH * QPK * HD).astype(jnp.bfloat16)


def draw_pattern(key, part):
    span_size = max(WIN, KSEL - 1)
    raw_scores = jax.random.randint(key, (NB, span_size), 0, 1 << 20)
    distinct = raw_scores * span_size + jnp.arange(span_size, dtype=jnp.int32)[None, :]
    order = jnp.argsort(distinct, axis=1)
    offsets = order[:, :KSEL - 1].astype(jnp.int32) + 1
    block_ids = jnp.arange(NB, dtype=jnp.int32)
    picks = block_ids[:, None] - offsets
    picks = jnp.where((offsets <= WIN) & (picks >= 0), picks, -1)
    return jnp.concatenate([block_ids[:, None], picks], axis=1).astype(jnp.int32)


def draw_log_decay(key, part):
    reference_speed = head_speeds(key)
    inner = jax.random.fold_in(key, 9)
    rough_key, place_key, loss_key = jax.random.split(inner, 3)
    rough_approximation = jnp.exp(jax.random.uniform(rough_key, (MH, TOKENS), minval=-0.7, maxval=0.7))
    placement_sequence = jax.random.randint(place_key, (2,), 0, TOKENS)
    objective_numbers = jax.random.uniform(loss_key, (MH, 2), minval=0.2, maxval=0.5)
    offset_indices = jnp.arange(TOKENS)
    spike_occurrences = jnp.where(offset_indices[None, :] == placement_sequence[0], jnp.log1p(-objective_numbers[:, 0:1]), 0.0)
    spike_occurrences = spike_occurrences + jnp.where(offset_indices[None, :] == placement_sequence[1], jnp.log1p(-objective_numbers[:, 1:2]), 0.0)
    return (-reference_speed[:, None] * rough_approximation + spike_occurrences).astype(jnp.float32)


def draw_x_in(key, part):
    reference_speed = head_speeds(key)
    inner = jax.random.fold_in(key, 13)
    noise = jnp.clip(jax.random.normal(inner, (TOKENS, MH, P_SIZE)), -6.0, 6.0)
    scaled = noise * jnp.sqrt(2.0 * reference_speed)[None, :, None]
    return scaled.reshape(TOKENS, MH * P_SIZE).astype(jnp.bfloat16)


def shard_levels(stream_key, dims, cuts, low, high):
    level = 1.0
    for axis_at, blocks in cuts:
        steps = jax.random.uniform(jax.random.fold_in(jax.random.fold_in(stream_key, 6), axis_at), (blocks,), jnp.float32, low / len(cuts), high / len(cuts))
        level = level * jnp.repeat(jnp.exp(steps), dims[axis_at] // blocks).reshape((-1,) + (1,) * (len(dims) - 1 - axis_at))
    return level


def centred(stream_key, dims, scale, reach, cuts=(), held_as=jnp.bfloat16):
    entries = scale * jax.random.normal(stream_key, dims, jnp.float32)
    if cuts:
        entries = entries * shard_levels(stream_key, dims, cuts, -0.22, 0.18)
    return jnp.clip(entries, -reach, reach).astype(held_as)


def setup_inputs(seed: int = 0, part: int = 0) -> dict:
    seeds = jax.random.split(jax.random.key(seed), 11)
    own_keys = jax.random.split(jax.random.fold_in(seeds[10], part), 11)
    queries = draw_queries(jax.random.fold_in(jax.random.fold_in(seeds[10], part), 71), part)
    keys = draw_keys(jax.random.fold_in(jax.random.fold_in(seeds[10], part), 71), part)
    values = centred(own_keys[2], (TOKENS, KVH * HD), 1.0, 6.0, ((0, 8), (1, 2)))
    pattern = draw_pattern(jax.random.fold_in(jax.random.fold_in(seeds[10], part), 71), part)
    x_in = draw_x_in(jax.random.fold_in(jax.random.fold_in(seeds[10], part), 71), part)
    z_gate = centred(own_keys[5], (TOKENS, MH * P_SIZE), 1.0, 6.0, ((0, 8), (1, 2)))
    bmat = centred(own_keys[6], (TOKENS, SG * N), 1.0, 6.0, ((0, 8), (1, 2)))
    cmat = centred(own_keys[7], (TOKENS, SG * N), N ** -0.5, 0.5, ((0, 8), (1, 2)))
    log_decay = draw_log_decay(jax.random.fold_in(jax.random.fold_in(seeds[10], part), 71), part)
    gain = jnp.clip(1.0 + 0.18 * jax.random.normal(seeds[9], (MH * P_SIZE,), jnp.float32), 0.1, 1.9)
    return {"queries": queries, "keys": keys, "values": values, "pattern": pattern, "x_in": x_in, "z_gate": z_gate, "bmat": bmat, "cmat": cmat, "log_decay": log_decay, "gain": gain}


def ssd_block(state_in, inputs):
    x_vals, b_vals, c_vals, log_rates = inputs
    cumulative = jnp.cumsum(log_rates, axis=-1)
    length = cumulative.shape[-1]
    spread = cumulative[..., :, None] - cumulative[..., None, :]
    lower_tri = jnp.tril(jnp.ones((length, length), dtype=bool))
    decays = jnp.exp(jnp.where(lower_tri, spread, -jnp.inf))
    affinity = jnp.einsum('lgn,mgn->glm', c_vals, b_vals, precision=lax.Precision.HIGHEST)
    inside = jnp.einsum('glm,ghlm,mghp->lghp', affinity, decays, x_vals, precision=lax.Precision.HIGHEST)
    carried = jnp.einsum('lgn,ghpn->lghp', c_vals, state_in, precision=lax.Precision.HIGHEST)
    carried = carried * jnp.transpose(jnp.exp(cumulative), (2, 0, 1))[..., None]
    weights = jnp.exp(cumulative[..., -1:] - cumulative)
    summary = jnp.einsum('ghl,lghp,lgn->ghpn', weights, x_vals, b_vals, precision=lax.Precision.HIGHEST)
    state_out = jnp.exp(cumulative[..., -1])[..., None, None] * state_in + summary
    return (state_out, inside + carried)

def gate_scaled_rmsnorm(mixed_rows, z_gate, gain):
    gated_rows = mixed_rows * jax.nn.silu(z_gate.astype(jnp.float32))
    row_count = gated_rows.shape[0]
    grouped = gated_rows.reshape(row_count, -1, HG * P_SIZE)
    inverse_rms = lax.rsqrt(lax.optimization_barrier(jnp.mean(grouped * grouped, axis=-1, keepdims=True)) + 1e-05)
    scaled = grouped * inverse_rms * gain.reshape(-1, HG * P_SIZE)
    return scaled.reshape(row_count, -1).astype(jnp.bfloat16)

def attention(queries, keys, values, pattern):
    q_blocks = queries.astype(jnp.float32).reshape(NB, BLK, KVH, QPK, HD)
    k_blocks = keys.astype(jnp.float32).reshape(NB, BLK, KVH, HD)
    v_blocks = values.astype(jnp.float32).reshape(NB, BLK, KVH, HD)

    def one_block(inputs):
        q_rows, listed, block_no = inputs
        clipped = jnp.clip(listed, 0, NB - 1)
        key_sel = k_blocks[clipped].reshape(KSEL * BLK, KVH, HD)
        value_sel = v_blocks[clipped].reshape(KSEL * BLK, KVH, HD)
        scores = jnp.einsum('qkgd,mkd->kgqm', q_rows, key_sel) * HD ** (-0.5)
        key_pos = (listed[:, None] * BLK + jnp.arange(BLK, dtype=jnp.int32)[None, :]).reshape(-1)
        query_pos = block_no * BLK + jnp.arange(BLK, dtype=jnp.int32)
        usable = jnp.repeat(listed >= 0, BLK)
        allowed = usable[None, :] & (key_pos[None, :] <= query_pos[:, None])
        scores = jnp.where(allowed, scores, -jnp.inf)
        row_max = lax.optimization_barrier(jnp.max(scores, axis=-1, keepdims=True))
        expo = jnp.exp(scores - row_max)
        row_total = lax.optimization_barrier(jnp.sum(expo, axis=-1))
        rounded = lax.optimization_barrier(expo.astype(jnp.bfloat16)).astype(jnp.float32)
        mixed_rows = jnp.einsum('kgqm,mkd->qkgd', rounded, value_sel)
        mixed_rows = mixed_rows / jnp.transpose(row_total, (2, 0, 1))[..., None]
        return mixed_rows.reshape(BLK, KVH * QPK * HD)
    result = lax.map(one_block, (q_blocks, pattern, jnp.arange(NB, dtype=jnp.int32)))
    return result.reshape(TOKENS, KVH * QPK * HD).astype(jnp.bfloat16)

def reference(queries, keys, values, pattern, x_in, z_gate, bmat, cmat, log_decay, gain):
    block_count = TOKENS // SCAN_BLK
    x_vals = x_in.astype(jnp.float32).reshape(block_count, SCAN_BLK, SG, HG, P_SIZE)
    b_vals = bmat.astype(jnp.float32).reshape(block_count, SCAN_BLK, SG, N)
    c_vals = cmat.astype(jnp.float32).reshape(block_count, SCAN_BLK, SG, N)
    log_rates = jnp.transpose(log_decay.reshape(SG, HG, block_count, SCAN_BLK), (2, 0, 1, 3))
    zero_state = jnp.zeros((SG, HG, P_SIZE, N), jnp.float32)
    last_state, outputs = lax.scan(ssd_block, zero_state, (x_vals, b_vals, c_vals, log_rates))
    mixed_rows = outputs.reshape(TOKENS, MH * P_SIZE)
    ssm_out = gate_scaled_rmsnorm(mixed_rows, z_gate, gain)
    attn_out = attention(queries, keys, values, pattern)
    return (attn_out, ssm_out)
```

```python
import jax
import jax.numpy as jnp
from jax import lax
from jax.experimental import pallas as pl
from jax.experimental.pallas import tpu as pltpu
from jax.sharding import PartitionSpec as P

BLK = 128
HD = 128
P_SIZE = 64
N = 128
EPS = 1e-05
F32 = jnp.float32
BF16 = jnp.bfloat16
HIGHEST = lax.Precision.HIGHEST
EXTRA = 16


def whole(count):
    return [pl.BlockSpec(memory_space=pltpu.VMEM)] * count


def dot(a, b, dims=((1,), (0,)), precision=None):
    return lax.dot_general(a, b, (dims, ((), ())), precision=precision, preferred_element_type=F32)


def iota(shape, axis):
    return lax.broadcasted_iota(jnp.int32, shape, axis)


def per_channel(per_head, heads):
    width = heads * P_SIZE
    spread = jnp.where(iota((heads, width), 1) // P_SIZE == iota((heads, width), 0), 1.0, 0.0).astype(BF16)
    upper = per_head.astype(BF16)
    lower = (per_head - upper.astype(F32)).astype(BF16)
    return dot(upper, spread) + dot(lower, spread)


def decay_row(ref):
    tail = ref[N : N + EXTRA, :].astype(F32)
    return tail[0:1] + tail[EXTRA // 2 : EXTRA // 2 + 1]


def with_decay(ref, decay):
    upper = decay.astype(BF16).astype(F32)
    ref[N : N + EXTRA, :] = jnp.concatenate([upper, decay - upper], axis=0).astype(BF16)


def summary_kernel(x_ref, b_ref, rate_ref, k_ref, v_ref, state_ref, kv_ref):
    rates = rate_ref[...]
    heads, length = rates.shape
    later = jnp.where(iota((length, length), 1) > iota((length, length), 0), 1.0, 0.0)
    to_end = dot(later, rates, ((1,), (1,)), HIGHEST)
    weighted = x_ref[...].astype(F32) * per_channel(jnp.exp(to_end), heads)
    state = dot(b_ref[...], weighted.astype(BF16), ((0,), (0,)))
    state_ref[0:N, :] = state.astype(BF16)
    total = dot(jnp.ones((8, length), F32), rates, ((1,), (1,)), HIGHEST)
    with_decay(state_ref, per_channel(jnp.exp(total), heads))
    kv_ref[0:BLK, :] = k_ref[...]
    kv_ref[BLK : 2 * BLK, :] = v_ref[...]


def combine_kernel(bit, mine_ref, other_ref, out_ref):
    mine, other = decay_row(mine_ref), decay_row(other_ref)
    is_later = (lax.axis_index("ctx") & bit) != 0
    keep = jnp.where(is_later, jnp.ones_like(other), other)
    take = jnp.where(is_later, mine, jnp.ones_like(mine))
    state = keep * mine_ref[0:N, :].astype(F32) + take * other_ref[0:N, :].astype(F32)
    out_ref[0:N, :] = state.astype(BF16)
    with_decay(out_ref, jnp.broadcast_to(mine * other, (8, mine.shape[1])))


def inside_kernel(bits, x_ref, b_ref, c_ref, rate_ref, z_ref, *refs):
    received, (base_ref, factor_ref) = refs[:-2], refs[-2:]
    rates = rate_ref[...]
    heads, length = rates.shape
    row, col = iota((length, length), 0), iota((length, length), 1)
    upto = jnp.where(col <= row, 1.0, 0.0)
    cum_cols = dot(upto, rates, ((1,), (1,)), HIGHEST)
    cum_rows = dot(rates, upto, ((1,), (1,)), HIGHEST)
    c_half = c_ref[...]
    affinity = dot(c_half, b_ref[...], ((1,), (1,)))
    parts = []
    for head in range(heads):
        spread = cum_cols[:, head : head + 1] - cum_rows[head : head + 1, :]
        mixing = affinity * jnp.exp(jnp.where(col <= row, spread, -jnp.inf))
        parts.append(dot(mixing.astype(BF16), x_ref[:, head * P_SIZE : (head + 1) * P_SIZE]))
    inside = jnp.concatenate(parts, axis=1)
    position = lax.axis_index("ctx")
    since = jnp.ones((1, heads * P_SIZE), F32)
    carried = jnp.zeros((length, heads * P_SIZE), F32)
    for bit, ref in zip(bits, received):
        is_later = (position & bit) != 0
        share = jnp.where(is_later, since, jnp.zeros_like(since))
        carried = carried + dot(c_half, ref[0:N, :]) * share
        since = jnp.where(is_later, since * decay_row(ref), since)
    reach = per_channel(jnp.exp(cum_cols), heads)
    z = z_ref[...].astype(F32)
    gate = z / (1.0 + jnp.exp(-z))
    base_ref[...] = (inside + carried * reach) * gate
    last = jnp.where((position & bits[-1]) != 0, since, jnp.zeros_like(since))
    factor_ref[...] = reach * last * gate


def finish_kernel(c_ref, state_ref, base_ref, factor_ref, gain_ref, out_ref):
    gated = base_ref[...] + factor_ref[...] * dot(c_ref[...], state_ref[0:N, :])
    inverse = lax.rsqrt(jnp.mean(gated * gated, axis=-1, keepdims=True) + EPS)
    out_ref[...] = (gated * inverse * gain_ref[...]).astype(BF16)


def attention_kernel(pattern_ref, q_ref, own_ref, two_ref, cross_ref, third_ref, pair_ref, out_ref):
    position = lax.axis_index("ctx")
    even = (position & 1) == 0

    def listed(block):
        hit = pattern_ref[0, 1] == block
        for entry in range(2, pattern_ref.shape[1]):
            hit = hit | (pattern_ref[0, entry] == block)
        return hit & (block >= 0)

    blocks = [position - 2, (position ^ 1) - 2, jnp.where(even, position - 3, position - 1)]
    last = jnp.where(even, third_ref[...], pair_ref[...])
    sources = [own_ref[...], two_ref[...], cross_ref[...], last]
    members = q_ref.shape[1] // own_ref.shape[1]
    rows = members * BLK
    causal = iota((rows, BLK), 1) <= (iota((rows, BLK), 0) & (BLK - 1))
    for kv_head in range(own_ref.shape[1] // HD):
        cols = slice(kv_head * HD, (kv_head + 1) * HD)
        at = [(kv_head * members + member) * HD for member in range(members)]
        q = jnp.concatenate([q_ref[:, a : a + HD] for a in at], axis=0)
        scores = []
        for order, source in enumerate(sources):
            part = dot(q, source[0:BLK, cols], ((1,), (1,))) * HD ** (-0.5)
            keep = causal if order == 0 else listed(blocks[order - 1])
            scores.append(jnp.where(keep, part, -jnp.inf))
        scores = jnp.concatenate(scores, axis=1)
        expo = jnp.exp(scores - jnp.max(scores, axis=-1, keepdims=True))
        total = jnp.sum(expo, axis=-1, keepdims=True)
        values = jnp.concatenate([source[BLK : 2 * BLK, cols] for source in sources], axis=0)
        mixed = dot(expo.astype(BF16), values) / total
        for member, a in enumerate(at):
            out_ref[:, a : a + HD] = mixed[member * BLK : (member + 1) * BLK].astype(BF16)


def call(kernel, out, *args, flops=1000000, moved=1000000, specs=None):
    return pl.pallas_call(
        kernel,
        out_shape=out,
        in_specs=specs or whole(len(args)),
        out_specs=jax.tree.map(lambda _: pl.BlockSpec(memory_space=pltpu.VMEM), out),
        cost_estimate=pl.CostEstimate(flops=flops, bytes_accessed=moved, transcendentals=0),
    )(*args)


def on_device(queries, keys, values, pattern, x_in, z_gate, bmat, cmat, log_decay, gain):
    count = lax.axis_size("ctx")
    tokens, width = x_in.shape
    bits = [1 << power for power in range((count - 1).bit_length())]
    shape = jax.ShapeDtypeStruct
    state_shape = shape((N + EXTRA, width), BF16)

    def swapped(value, bit):
        return lax.ppermute(value, "ctx", [(k, k ^ bit) for k in range(count)])

    state, kv = call(
        summary_kernel,
        (state_shape, shape((2 * BLK, keys.shape[1]), BF16)),
        x_in, bmat, log_decay, keys, values,
    )
    two = lax.ppermute(kv, "ctx", [(k, (k + 2) % count) for k in range(count)])
    pair = swapped(kv, 1)
    cross = swapped(two, 1)
    ends = [(0, 0), (count - 1, count - 1)]
    inner = [(k, k + 1 if k % 2 else k - 1) for k in range(1, count - 1)]
    third = lax.ppermute(two, "ctx", ends + inner)

    received = []
    for order, bit in enumerate(bits):
        other = swapped(state, bit)
        received.append(other)
        if order + 1 < len(bits):
            state = call(lambda *refs, bit=bit: combine_kernel(bit, *refs), state_shape, state, other)

    wide = shape((tokens, width), F32)
    base, factor = call(
        lambda *refs: inside_kernel(bits, *refs), (wide, wide),
        x_in, bmat, cmat, log_decay, z_gate, *received[:-1],
    )
    attn_out = call(
        attention_kernel, shape(queries.shape, BF16),
        pattern, queries, kv, two, cross, third, pair,
        specs=[pl.BlockSpec(memory_space=pltpu.SMEM)] + whole(6),
    )
    ssm_out = call(
        finish_kernel, shape((tokens, width), BF16),
        cmat, received[-1], base, factor, gain.reshape(1, width),
    )
    return (attn_out, ssm_out)


def solution(mesh):
    rows = P(("groups", "ctx"), "head")
    placed = (rows, rows, rows, P(("groups", "ctx"), None), rows, rows, rows, rows, P(("groups", "head"), "ctx"), P("head"))
    return jax.shard_map(on_device, mesh=mesh, in_specs=placed, out_specs=(rows, rows), check_vma=False)
```
